32 devices in a mesh: dom: 16 (over z, y, core), rep: 2 (over x).
Axes of the slice: x: 2, y: 2, z: 4, core: 2. Of those that a mesh axis runs over, the one named last changes fastest.
Arguments:
- node_feats: bfloat16 [4096, 400], P('dom'), may hold values from -6 to 6
- w_self: bfloat16 [400, 400], replicated, may hold values from -0.3125 to 0.3125
- w_neigh: bfloat16 [400, 400], replicated, may hold values from -0.3125 to 0.3125
- neighbour_index: int32 [4096, 10], P('dom'), may hold values from 0 to 383, as said below
- neighbour_count: int32 [4096], P('dom'), may hold values from 1 to 10
- send_index: int32 [16, 16, 8], P('dom'), may hold values from 0 to 255
- send_count: int32 [16, 16], P('dom'), may hold values from 0 to 8
- edge_src: int32 [16, 5, 512], P('dom', None, 'rep'), may hold values from 0 to 255
- edge_dst: int32 [16, 5, 512], P('dom', None, 'rep'), may hold values from 0 to 255
- tile_count: int32 [16, 5, 4], P('dom', None, 'rep'), may hold values from 1 to 128, as said below
- neg_rows: int32 [16, 5, 512], P('dom'), may hold values from 0 to 255
Outputs:
- loss: float32 [], replicated
- grad_x: float32 [4096, 400], P('dom')
- grad_self: float32 [400, 400], replicated
- grad_neigh: float32 [400, 400], replicated
The draws below stay inside these ranges and needn't reach their ends.
Inputs may be any that keep to these rules, and one draw needn't show every extreme that they name: `neighbour_index`: a value below 256 is a node of the own partition; a value 256 + s * 8 + c is slot c of sender s, which holds zeros when c >= send_count[s, p]; slots at or beyond neighbour_count are ignored. `tile_count`: every bucket has at least one full tile.
All inputs are finite; a program needn't handle non-finite values.
Results may differ from the reference program's by a relative error of at most 0.0035.
Values may be sent and summed in bfloat16 or wider, within the bound.
A program may use at most 64 MiB of HBM per device.

```python
import jax
import jax.numpy as jnp
from jax import lax

D = 400
NODE_DEV = 256
FANOUT = 10
CAP = 8
NEG = 512
HALF = 2
PARTS_SIZE = 16
NODES = 4096
WINDOW = 5
EDGES = 512
TILES = 4
TABLE = 384


def draw_neighbour_index(key, part):
    key_local, key_remote, key_pick = jax.random.split(key, 3)
    local = jax.random.randint(key_local, (NODES, FANOUT), 0, NODE_DEV)
    remote = NODE_DEV + jax.random.randint(key_remote, (NODES, FANOUT), 0, PARTS_SIZE * CAP)
    pick = jax.random.randint(key_pick, (NODES, FANOUT), 0, 2)
    return jnp.where(pick == 1, remote, local).astype(jnp.int32)


def draw_send_count(key, part):
    counts = jax.random.randint(key, (PARTS_SIZE, PARTS_SIZE), 0, CAP + 1)
    sender = jnp.arange(PARTS_SIZE)[:, None]
    receiver = jnp.arange(PARTS_SIZE)[None, :]
    full = receiver == (sender + 1) % PARTS_SIZE
    return jnp.where(full, CAP, counts).astype(jnp.int32)


def draw_tile_count(key, part):
    key_low, key_fill, key_pos = jax.random.split(key, 3)
    lowest = jax.random.randint(key_low, (PARTS_SIZE, WINDOW, 1), 1, 129)
    raw = jax.random.randint(key_fill, (PARTS_SIZE, WINDOW, TILES), 0, 129)
    filled = lowest + raw * (129 - lowest) // 129
    where_full = jax.random.randint(key_pos, (PARTS_SIZE, WINDOW, 1), 0, TILES)
    tiles_here = jnp.arange(TILES)[None, None, :]
    return jnp.where(tiles_here == where_full, 128, jnp.minimum(filled, 128)).astype(jnp.int32)


def with_ends(drawn, key, smallest, high):
    longest = drawn.shape.index(max(drawn.shape))
    spots = []
    for shift in (0, 1):
        where = [jax.random.randint(jax.random.fold_in(key, axis), (), 0, length) for axis, length in enumerate(drawn.shape)]
        where[longest] = (where[longest] + shift) % drawn.shape[longest]
        spots.append(tuple(where))
    return drawn.at[spots[0]].set(smallest).at[spots[1]].set(high)


def shard_levels(rng, extent, cuts, smallest, top_value):
    level = 1.0
    for dim, blocks in cuts:
        heights = jax.random.uniform(jax.random.fold_in(jax.random.fold_in(rng, 6), dim), (blocks,), jnp.float32, smallest / len(cuts), top_value / len(cuts))
        level = level * jnp.repeat(jnp.exp(heights), extent[dim] // blocks).reshape((-1,) + (1,) * (len(extent) - 1 - dim))
    return level


def bell_draw(key, dims, scale, bound, cuts=(), kind=jnp.bfloat16):
    result = scale * jax.random.normal(key, dims, jnp.float32)
    if cuts:
        result = result * shard_levels(key, dims, cuts, -0.22, 0.18)
    return jnp.clip(result, -bound, bound).astype(kind)


def setup_inputs(seed: int = 0) -> dict:
    seeds = jax.random.split(jax.random.key(seed), 12)
    node_feats = bell_draw(seeds[0], (NODES, D), 1.0, 6.0, ((0, 16),))
    w_self = bell_draw(seeds[1], (D, D), D ** -0.5, 0.3125)
    w_neigh = bell_draw(seeds[2], (D, D), D ** -0.5, 0.3125)
    neighbour_index = draw_neighbour_index(jax.random.fold_in(seeds[11], 71), 0)
    neighbour_count = with_ends(jax.random.randint(seeds[4], (NODES,), 1, FANOUT + 1), jax.random.fold_in(seeds[4], 1), 1, FANOUT).astype(jnp.int32)
    send_index = with_ends(jax.random.randint(seeds[5], (PARTS_SIZE, PARTS_SIZE, CAP), 0, NODE_DEV), jax.random.fold_in(seeds[5], 1), 0, NODE_DEV - 1).astype(jnp.int32)
    send_count = draw_send_count(jax.random.fold_in(seeds[11], 71), 0)
    edge_src = with_ends(jax.random.randint(seeds[7], (PARTS_SIZE, WINDOW, EDGES), 0, NODE_DEV), jax.random.fold_in(seeds[7], 1), 0, NODE_DEV - 1).astype(jnp.int32)
    edge_dst = with_ends(jax.random.randint(seeds[8], (PARTS_SIZE, WINDOW, EDGES), 0, NODE_DEV), jax.random.fold_in(seeds[8], 1), 0, NODE_DEV - 1).astype(jnp.int32)
    tile_count = draw_tile_count(jax.random.fold_in(seeds[11], 71), 0)
    neg_rows = with_ends(jax.random.randint(seeds[10], (PARTS_SIZE, WINDOW, NEG), 0, NODE_DEV), jax.random.fold_in(seeds[10], 1), 0, NODE_DEV - 1).astype(jnp.int32)
    return {"node_feats": node_feats, "w_self": w_self, "w_neigh": w_neigh, "neighbour_index": neighbour_index, "neighbour_count": neighbour_count, "send_index": send_index, "send_count": send_count, "edge_src": edge_src, "edge_dst": edge_dst, "tile_count": tile_count, "neg_rows": neg_rows}


negative_weight = 0.03125


def edge_terms(own, visitor, sources, targets, filled, negatives):
    edge_total = sources.shape[0]
    scale = own.shape[1] ** -0.5
    position = jnp.arange(edge_total, dtype=jnp.int32)
    live = ((position % 128) < jnp.repeat(filled, 128, total_repeat_length=edge_total)).astype(jnp.float32)
    src_emb = own[sources]
    dst_emb = visitor[targets]
    neg_emb = visitor[negatives]
    positive = jnp.sum(src_emb.astype(jnp.float32) * dst_emb.astype(jnp.float32), axis=1) * scale
    negative = lax.dot_general(src_emb, neg_emb, (((1,), (1,)), ((), ())), preferred_element_type=jnp.float32) * scale
    loss_part = jnp.sum(live * (jax.nn.softplus(-positive) + negative_weight * jnp.sum(jax.nn.softplus(negative), axis=1)))
    pos_grad = -live * jax.nn.sigmoid(-positive)
    neg_grad = (live[:, None] * negative_weight * jax.nn.sigmoid(negative)).astype(jnp.bfloat16)
    src_grad = scale * (pos_grad[:, None] * dst_emb.astype(jnp.float32) + jnp.dot(neg_grad, neg_emb, preferred_element_type=jnp.float32))
    dst_grad = scale * pos_grad[:, None] * src_emb.astype(jnp.float32)
    neg_back = scale * lax.dot_general(neg_grad, src_emb, (((0,), (0,)), ((), ())), preferred_element_type=jnp.float32)
    home = jnp.zeros(own.shape, jnp.float32).at[sources].add(src_grad)
    visiting = jnp.zeros(visitor.shape, jnp.float32).at[targets].add(dst_grad).at[negatives].add(neg_back)
    return loss_part, home, visiting


def reference(node_feats, w_self, w_neigh, neighbour_index, neighbour_count, send_index, send_count, edge_src, edge_dst, tile_count, neg_rows):
    blocks = node_feats.reshape(PARTS_SIZE, NODE_DEV, D)
    slot_ids = jnp.arange(CAP, dtype=jnp.int32)
    owners = jnp.arange(PARTS_SIZE, dtype=jnp.int32)
    index_blocks = neighbour_index.reshape(PARTS_SIZE, NODE_DEV, FANOUT)
    count_blocks = neighbour_count.reshape(PARTS_SIZE, NODE_DEV)
    fan_ids = jnp.arange(FANOUT, dtype=jnp.int32)

    def mean_for(part):
        picks = send_index[:, part, :]
        live = slot_ids[None, :] < send_count[:, part][:, None]
        got = blocks[owners[:, None], picks]
        got = jnp.where(live[:, :, None], got, jnp.zeros((), jnp.bfloat16))
        lookup = jnp.concatenate([blocks[part], got.reshape(PARTS_SIZE * CAP, D)], axis=0)
        counts = count_blocks[part]
        valid = (fan_ids[None, :] < counts[:, None]).astype(jnp.float32)
        rows_here = lookup[index_blocks[part]].astype(jnp.float32) * valid[:, :, None]
        return (jnp.sum(rows_here, axis=1) / counts[:, None].astype(jnp.float32)).astype(jnp.bfloat16)

    neighbour_mean = lax.map(mean_for, owners).reshape(NODES, D)
    hidden = (jnp.dot(node_feats, w_self, preferred_element_type=jnp.float32) + jnp.dot(neighbour_mean, w_neigh, preferred_element_type=jnp.float32)).astype(jnp.bfloat16)
    hidden_blocks = hidden.reshape(PARTS_SIZE, NODE_DEV, D)
    grad_hidden = jnp.zeros((PARTS_SIZE, NODE_DEV, D), jnp.float32)
    total = jnp.zeros((), jnp.float32)
    for slot in range(WINDOW):
        offset = slot - HALF
        visitors = jnp.roll(hidden_blocks, -offset, axis=0)

        def per_part(items):
            return edge_terms(items[0], items[1], items[2], items[3], items[4], items[5])

        losses, homes, visits = lax.map(per_part, (hidden_blocks, visitors, edge_src[:, slot], edge_dst[:, slot], tile_count[:, slot], neg_rows[:, slot]))
        total = total + jnp.sum(losses)
        grad_hidden = grad_hidden + homes + jnp.roll(visits, offset, axis=0)
    grad_b = grad_hidden.reshape(NODES, D).astype(jnp.bfloat16)
    direct = jnp.dot(grad_b, w_self.T, preferred_element_type=jnp.float32)
    grad_mean = (jnp.dot(grad_b, w_neigh.T, preferred_element_type=jnp.float32) / neighbour_count[:, None].astype(jnp.float32)).astype(jnp.bfloat16)
    mean_blocks = grad_mean.reshape(PARTS_SIZE, NODE_DEV, D)

    def spread(carry, part):
        counts = count_blocks[part]
        valid = fan_ids[None, :] < counts[:, None]
        pieces = jnp.where(valid[:, :, None], mean_blocks[part][:, None, :].astype(jnp.float32), jnp.zeros((), jnp.float32))
        contrib = jnp.zeros((TABLE, D), jnp.float32).at[index_blocks[part]].add(pieces)
        carry = carry.at[part].add(contrib[:NODE_DEV])
        remote = contrib[NODE_DEV:].reshape(PARTS_SIZE, CAP, D)
        live = slot_ids[None, :] < send_count[:, part][:, None]
        remote = jnp.where(live[:, :, None], remote, jnp.zeros((), jnp.float32))
        carry = carry.at[owners[:, None], send_index[:, part, :]].add(remote)
        return carry, None

    spread_sum, unused = lax.scan(spread, jnp.zeros((PARTS_SIZE, NODE_DEV, D), jnp.float32), owners)
    grad_x = direct + spread_sum.reshape(NODES, D)
    scale = float(NODES) ** -0.5
    grad_self = jnp.dot(node_feats.T, grad_b, preferred_element_type=jnp.float32) * scale
    grad_neigh = jnp.dot(neighbour_mean.T, grad_b, preferred_element_type=jnp.float32) * scale
    loss = total / float(PARTS_SIZE * WINDOW * EDGES)
    return (loss, grad_x, grad_self, grad_neigh)
```

```python
import jax
import jax.numpy as jnp
from jax import lax
from jax.sharding import PartitionSpec as P

negative_weight = 0.03125
contract_last = (((1,), (1,)), ((), ()))
contract_first = (((0,), (0,)), ((), ()))


def from_behind(value, axis, steps):
    count = lax.axis_size(axis)
    pairs = [(source, (source + steps) % count) for source in range(count)]
    return lax.ppermute(value, axis, pairs)


def row_hits(rows, picks):
    ids = lax.broadcasted_iota(jnp.int32, (rows, picks.shape[0]), 0)
    return (ids == picks[None, :]).astype(jnp.bfloat16)


def bucket_counts(rows, sources, targets, negatives):
    src_hits = row_hits(rows, sources)
    dst_hits = row_hits(rows, targets)
    edge_count = lax.dot_general(
        src_hits, dst_hits, contract_last, preferred_element_type=jnp.float32
    )
    src_count = jnp.sum(src_hits.astype(jnp.float32), axis=1)
    neg_count = jnp.sum(row_hits(rows, negatives).astype(jnp.float32), axis=1)
    return edge_count, negative_weight * src_count[:, None] * neg_count[None, :]


def score_grad(own, visitor, counts, with_loss):
    edge_count, pair_count = counts
    scale = own.shape[1] ** (-0.5)
    score = (
        lax.dot_general(own, visitor, contract_last, preferred_element_type=jnp.float32) * scale
    )
    decay = jnp.exp(-jnp.abs(score))
    inverse = 1.0 / (1.0 + decay)
    high = inverse
    low = decay * inverse
    sig_pos = jnp.where(score >= 0, high, low)
    sig_neg = jnp.where(score >= 0, low, high)
    grad = ((pair_count * sig_pos - edge_count * sig_neg) * scale).astype(jnp.bfloat16)
    loss = None
    if with_loss:
        shared = jnp.log1p(decay)
        loss = jnp.sum(
            edge_count * (jnp.maximum(-score, 0.0) + shared)
            + pair_count * (jnp.maximum(score, 0.0) + shared)
        )
    return grad, loss


def on_device(
    node_feats,
    w_self,
    w_neigh,
    neighbour_index,
    neighbour_count,
    send_index,
    send_count,
    edge_src,
    edge_dst,
    tile_count,
    neg_rows,
):
    partitions = lax.axis_size("dom")
    replicas = lax.axis_size("rep")
    node_rows, width = node_feats.shape
    fan_out = neighbour_index.shape[1]
    slot_cap = send_index.shape[2]
    window = edge_src.shape[1]
    half_width = (window - 1) // 2
    edge_here = edge_src.shape[2]
    position = jnp.arange(edge_here, dtype=jnp.int32)
    live = position % 128 < jnp.repeat(
        tile_count[0], 128, axis=1, total_repeat_length=edge_here
    )
    live_src = jnp.where(live, edge_src[0], -1)
    packed = jnp.concatenate([live_src, edge_dst[0], neg_rows[0]], axis=1)
    visits = {}
    for offset in range(-half_width, half_width + 1):
        if offset:
            visits[offset] = from_behind(packed[offset + half_width], "dom", offset)
    slot_live = jnp.arange(slot_cap, dtype=jnp.int32)[None, :] < send_count[0][:, None]
    picks = jnp.where(slot_live, send_index[0], -1).reshape(-1)
    send_hits = row_hits(node_rows, picks)
    outgoing = lax.dot_general(
        send_hits, node_feats, contract_first, preferred_element_type=jnp.float32
    ).astype(jnp.bfloat16)
    incoming = lax.all_to_all(outgoing, "dom", split_axis=0, concat_axis=0, tiled=True)
    lookup_table = jnp.concatenate([node_feats, incoming], axis=0)
    columns = jnp.arange(lookup_table.shape[0], dtype=jnp.int32)
    counts_f = neighbour_count.astype(jnp.float32)[:, None]
    adjacency = jnp.zeros((node_rows, lookup_table.shape[0]), jnp.float32)
    for which in range(fan_out):
        hits = (neighbour_index[:, which : which + 1] == columns[None, :]) & (
            which < neighbour_count
        )[:, None]
        adjacency = adjacency + hits.astype(jnp.float32)
    adjacency = adjacency.astype(jnp.bfloat16)
    neighbour_mean = (
        jnp.dot(adjacency, lookup_table, preferred_element_type=jnp.float32) / counts_f
    ).astype(jnp.bfloat16)
    hidden = (
        jnp.dot(node_feats, w_self, preferred_element_type=jnp.float32)
        + jnp.dot(neighbour_mean, w_neigh, preferred_element_type=jnp.float32)
    ).astype(jnp.bfloat16)
    home = jnp.zeros((node_rows, width), jnp.float32)
    loss_sum = jnp.zeros((), jnp.float32)

    def split(row):
        return row[:edge_here], row[edge_here : 2 * edge_here], row[2 * edge_here :]

    for offset in (0, 1, -1, 2, -2):
        own_counts = bucket_counts(node_rows, *split(packed[offset + half_width]))
        visitor = hidden if offset == 0 else from_behind(hidden, "dom", -offset)
        grad, loss = score_grad(hidden, visitor, own_counts, True)
        loss_sum = loss_sum + loss
        home = home + jnp.dot(grad, visitor, preferred_element_type=jnp.float32)
        if offset == 0:
            home = home + lax.dot_general(
                grad, hidden, contract_first, preferred_element_type=jnp.float32
            )
        else:
            back = bucket_counts(node_rows, *split(visits[-offset]))
            back_grad, unused = score_grad(visitor, hidden, back, False)
            home = home + lax.dot_general(
                back_grad, visitor, contract_first, preferred_element_type=jnp.float32
            )
    home_total, loss_total = lax.psum((home, loss_sum), "rep")
    grad_b = home_total.astype(jnp.bfloat16)
    scale = float(node_rows * partitions) ** (-0.5)
    self_part = (
        lax.dot_general(node_feats, grad_b, contract_first, preferred_element_type=jnp.float32)
        * scale
    )
    neigh_part = (
        lax.dot_general(
            neighbour_mean, grad_b, contract_first, preferred_element_type=jnp.float32
        )
        * scale
    )
    grad_self, grad_neigh, loss_all = lax.psum((self_part, neigh_part, loss_total), "dom")
    direct = lax.dot_general(grad_b, w_self, contract_last, preferred_element_type=jnp.float32)
    grad_mean = (
        lax.dot_general(grad_b, w_neigh, contract_last, preferred_element_type=jnp.float32)
        / counts_f
    ).astype(jnp.bfloat16)
    table_grad = lax.dot_general(
        adjacency, grad_mean, contract_first, preferred_element_type=jnp.float32
    )
    returned = lax.all_to_all(
        table_grad[node_rows:].astype(jnp.bfloat16),
        "dom",
        split_axis=0,
        concat_axis=0,
        tiled=True,
    )
    scattered = jnp.dot(send_hits, returned, preferred_element_type=jnp.float32)
    grad_x = direct + table_grad[:node_rows] + scattered
    loss = loss_all / float(partitions * window * edge_here * replicas)
    return (loss, grad_x, grad_self, grad_neigh)


def solution(mesh):
    in_specs = (
        P("dom", None),
        P(),
        P(),
        P("dom", None),
        P("dom"),
        P("dom", None, None),
        P("dom", None),
        P("dom", None, "rep"),
        P("dom", None, "rep"),
        P("dom", None, "rep"),
        P("dom", None, None),
    )
    out_specs = (P(), P("dom", None), P(), P())
    return jax.shard_map(
        on_device, mesh=mesh, in_specs=in_specs, out_specs=out_specs, check_vma=False
    )
```

```python
import functools

import jax
import jax.numpy as jnp
from jax import lax
from jax.experimental import pallas as pl
from jax.experimental.pallas import tpu as pltpu
from jax.sharding import PartitionSpec as P

negative_weight = 0.03125
F32 = jnp.float32
BF16 = jnp.bfloat16
MESH = pl.DeviceIdType.MESH


def dot_nn(a, b):
    return lax.dot_general(a, b, (((1,), (0,)), ((), ())), preferred_element_type=F32)


def dot_nt(a, b):
    return lax.dot_general(a, b, (((1,), (1,)), ((), ())), preferred_element_type=F32)


def dot_tn(a, b):
    return lax.dot_general(a, b, (((0,), (0,)), ((), ())), preferred_element_type=F32)


def row_hits(rows, picks):
    ids = lax.broadcasted_iota(jnp.int32, (rows, picks.shape[1]), 0)
    return jnp.where(ids == picks, 1.0, 0.0).astype(F32)


def step_kernel(
    parts,
    neg_parts,
    feats,
    w_self,
    w_neigh,
    nidx,
    nidx_t,
    count_f,
    pick_row,
    pick_col,
    packed,
    loss_out,
    gx_out,
    gs_out,
    gn_out,
    bnd_out,
    bnd_in,
    ret_out,
    ret_in,
    other,
    back,
    hid,
    vis,
    edge_own,
    edge_all,
    pair_own,
    pair_all,
    adj,
    adj_t,
    mean,
    lhs,
    rs_out,
    rs_in,
    full,
    loss_buf,
    home,
    bnd_s,
    bnd_r,
    ret_s,
    ret_r,
    mir_s,
    mir_r,
    idx_s,
    idx_r,
    hid_s,
    hid_r,
    rs_s,
    rs_r,
    ag_s,
    ag_r,
    fwd_s,
    fwd_r,
    los_s,
    los_r,
):
    me = lax.axis_index("dom")
    rep = lax.axis_index("rep")
    rows, width = feats.shape
    fan_out = nidx.shape[1]
    window, _, edge_here = packed.shape
    half = (window - 1) // 2
    owners, chunk = rs_out.shape[0], rs_out.shape[1]
    table = adj.shape[1]
    scale = width ** (-0.5)
    offsets = [o for o in range(-half, half + 1) if o]

    def at(shift):
        return lax.rem(me + shift + parts, parts)

    def copy(src, dst, s, r, dom, replica):
        return pltpu.make_async_remote_copy(
            src_ref=src,
            dst_ref=dst,
            send_sem=s,
            recv_sem=r,
            device_id=(dom, replica),
            device_id_type=MESH,
        )

    barrier = pltpu.get_barrier_semaphore()

    def greet(k, carry):
        pl.semaphore_signal(
            barrier, inc=1, device_id=(at(k), rep), device_id_type=MESH
        )
        return carry

    lax.fori_loop(1, parts, greet, 0)
    for o in range(-half, half + 1):
        pl.semaphore_signal(
            barrier, inc=1, device_id=(at(o), 1 - rep), device_id_type=MESH
        )

    lane = lax.broadcasted_iota(jnp.int32, (pick_col.shape[0], rows), 1)
    gather = jnp.where(lane == pick_col[...], 1.0, 0.0).astype(F32).astype(BF16)
    bnd_out[...] = dot_nn(gather, feats[...]).reshape(bnd_out.shape).astype(BF16)
    bnd_in[me] = bnd_out[me]

    pl.semaphore_wait(barrier, parts - 1 + window)

    def all_send(src_of, dst, s, r, limit=None):
        def send(k, carry):
            peer = at(k)

            def go():
                copy(src_of(peer), dst.at[me], s.at[peer], r.at[me], peer, rep).start()

            if limit is None:
                go()
            else:
                pl.when(peer < limit)(go)
            return carry

        lax.fori_loop(1, parts, send, 0)

    def all_recv(src_of, dst, s, r):
        def take(k, carry):
            peer = at(k)
            copy(src_of(peer), dst.at[peer], s.at[peer], r.at[peer], peer, rep).wait_recv()
            return carry

        lax.fori_loop(1, parts, take, 0)

    def all_done(src_of, dst, s, r, limit=None):
        def done(k, carry):
            peer = at(k)

            def go():
                copy(src_of(peer), dst.at[me], s.at[peer], r.at[me], peer, rep).wait_send()

            if limit is None:
                go()
            else:
                pl.when(peer < limit)(go)
            return carry

        lax.fori_loop(1, parts, done, 0)

    all_send(lambda k: bnd_out.at[k], bnd_in, bnd_s, bnd_r)
    mirror = copy(packed, other, mir_s, mir_r, me, 1 - rep)
    mirror.start()
    idx_copies = []
    for n, o in enumerate(offsets):
        for to in range(2):
            replica = rep if to == 0 else 1 - rep
            idx_copies.append(
                (
                    copy(
                        packed.at[o + half],
                        back.at[o + half, to],
                        idx_s.at[n, to],
                        idx_r.at[n, to],
                        at(o),
                        replica,
                    )
                )
            )
            idx_copies[-1].start()

    col_ids = lax.broadcasted_iota(jnp.int32, (rows, table), 1)
    total = jnp.zeros((rows, table), F32)
    for f in range(fan_out):
        total = total + jnp.where(col_ids == nidx[:, f : f + 1], 1.0, 0.0)
    adj[...] = total.astype(BF16)

    all_recv(lambda k: bnd_out.at[k], bnd_in, bnd_s, bnd_r)
    incoming = bnd_in[...].astype(F32).reshape(table - rows, width).astype(BF16)
    summed = dot_nn(adj[:, :rows], feats[...]) + dot_nn(adj[:, rows:], incoming)
    mean[...] = (summed / count_f[...]).astype(BF16)
    hid[...] = (dot_nn(feats[...], w_self[...]) + dot_nn(mean[...], w_neigh[...])).astype(BF16)
    hid_copies = {}
    for o in sorted(offsets, key=abs):
        w = o + half
        hid_copies[w] = copy(hid, vis.at[w], hid_s.at[w], hid_r.at[w], at(-o), rep)
        hid_copies[w].start()

    row_ids = lax.broadcasted_iota(jnp.int32, (table, rows), 0)
    total_t = jnp.zeros((table, rows), F32)
    for f in range(fan_out):
        total_t = total_t + jnp.where(row_ids == nidx_t[f : f + 1, :], 1.0, 0.0)
    adj_t[...] = total_t.astype(BF16)

    @pl.when(rep == 0)
    def _():
        lhs[...] = feats[...]

    @pl.when(rep != 0)
    def _():
        lhs[...] = mean[...]

    mirror.wait_recv()
    for c in idx_copies:
        c.wait_recv()
    ones = jnp.ones((8, edge_here), BF16)

    def counts(halves):
        return [
            (
                row_hits(rows, ref[w_, 0:1, :] if t is None else ref[w_, t, 0:1, :]),
                row_hits(rows, ref[w_, 1:2, :] if t is None else ref[w_, t, 1:2, :]),
            )
            for ref, w_, t in halves
        ]

    def neg_hits(ref, w_, t):
        out = []
        for n in range(neg_parts):
            row = ref[w_, 2 + n : 3 + n, :] if t is None else ref[w_, t, 2 + n : 3 + n, :]
            out.append(row_hits(rows, row))
        return out

    for w in range(window):
        o = w - half
        own = counts([(packed, w, None), (other, w, None)])
        if o == 0:
            from_there = own
            there_neg = (packed, w, None)
        else:
            v = window - 1 - w
            from_there = counts([(back, v, 0), (back, v, 1)])
            there_neg = (back, v, 0)
        e_own = jnp.zeros((rows, rows), F32)
        e_back = jnp.zeros((rows, rows), F32)
        c_own = jnp.zeros((rows, 1), F32)
        c_back = jnp.zeros((8, rows), F32)
        for src, dst in own:
            e_own = e_own + dot_nt(src.astype(BF16), dst.astype(BF16))
            c_own = c_own + jnp.sum(src, axis=1, keepdims=True)
        for src, dst in from_there:
            e_back = e_back + dot_nt(dst.astype(BF16), src.astype(BF16))
            c_back = c_back + dot_nt(ones, src.astype(BF16))
        d_own = jnp.zeros((8, rows), F32)
        for hits in neg_hits(packed, w, None):
            d_own = d_own + dot_nt(ones, hits.astype(BF16))
        d_back = jnp.zeros((rows, 1), F32)
        for hits in neg_hits(*there_neg):
            d_back = d_back + jnp.sum(hits, axis=1, keepdims=True)
        p_own = (negative_weight * c_own) * d_own[0:1, :]
        edge_own[w] = e_own
        edge_all[w] = e_own + e_back
        pair_own[w] = p_own
        pair_all[w] = p_own + (negative_weight * d_back) * c_back[0:1, :]

    loss_sum = jnp.zeros((1, 1), F32)
    for n, o in enumerate([0] + sorted(offsets, key=abs)):
        w = o + half
        if o == 0:
            visitor = hid[...]
        else:
            hid_copies[w].wait_recv()
            visitor = vis[w]
        score = dot_nt(hid[...], visitor) * scale
        decay = jnp.exp(-jnp.abs(score))
        inverse = 1.0 / (1.0 + decay)
        low = decay * inverse
        up = score >= 0
        sig_pos = jnp.where(up, inverse, low)
        sig_neg = jnp.where(up, low, inverse)
        grad = ((pair_all[w] * sig_pos - edge_all[w] * sig_neg) * scale).astype(BF16)
        shared = jnp.log1p(decay)
        terms = edge_own[w] * (jnp.maximum(-score, 0.0) + shared) + pair_own[w] * (
            jnp.maximum(score, 0.0) + shared
        )
        loss_sum = loss_sum + jnp.sum(
            jnp.sum(terms, axis=1, keepdims=True), axis=0, keepdims=True
        )
        add = dot_nn(grad, visitor)
        home[...] = add if n == 0 else home[...] + add

    grad_b = home[...].astype(BF16)
    loss_buf[me] = jnp.broadcast_to(loss_sum, loss_buf.shape[1:])

    weight_scale = float(rows * parts) ** (-0.5)
    part = dot_tn(lhs[...], grad_b) * weight_scale
    for k in range(owners):
        height = min(chunk, width - k * chunk)
        rs_out[k, :height, :] = part[k * chunk : k * chunk + height, :].astype(BF16)
        if height < chunk:
            rs_out[k, height:, :] = jnp.zeros((chunk - height, width), BF16)
    all_send(lambda k: rs_out.at[k], rs_in, rs_s, rs_r, owners)
    all_send(lambda k: loss_buf.at[me], loss_buf, los_s, los_r)

    direct = dot_nt(grad_b, w_self[...])
    grad_mean = (dot_nt(grad_b, w_neigh[...]) / count_f[...]).astype(BF16)
    ret_out[...] = dot_nn(adj_t[rows:, :], grad_mean).reshape(ret_out.shape).astype(BF16)
    ret_in[me] = ret_out[me]
    all_send(lambda k: ret_out.at[k], ret_in, ret_s, ret_r)
    gx_out[...] = direct + dot_nn(adj_t[:rows, :], grad_mean)

    @pl.when(me < owners)
    def _():
        rs_in[me] = rs_out[me]
        all_recv(lambda k: rs_out.at[me], rs_in, rs_s, rs_r)
        acc = lax.fori_loop(
            0,
            parts,
            lambda k, c: c + rs_in[k].astype(F32),
            jnp.zeros((chunk, width), F32),
        )
        full[rep, me] = acc.astype(BF16)

        def send(k, carry):
            peer = at(k)
            piece = full.at[rep, me]
            copy(piece, piece, ag_s.at[peer], ag_r.at[me], peer, rep).start()
            return carry

        lax.fori_loop(1, parts, send, 0)
        piece = full.at[rep, me]
        copy(piece, piece, fwd_s.at[me], fwd_r.at[me], me, 1 - rep).start()

    all_recv(lambda k: ret_out.at[k], ret_in, ret_s, ret_r)
    returned = ret_in[...].astype(F32).reshape(table - rows, width).astype(BF16)
    scatter = row_hits(rows, pick_row[...]).astype(BF16)
    gx_out[...] = gx_out[...] + dot_nn(scatter, returned)

    all_recv(lambda k: loss_buf.at[me], loss_buf, los_s, los_r)
    loss_out[...] = lax.fori_loop(
        0, parts, lambda k, c: c + loss_buf[k], jnp.zeros(loss_out.shape, F32)
    )

    def pass_on(k, carry):
        owner = at(k)

        @pl.when(owner < owners)
        def _():
            piece = full.at[rep, owner]
            copy(piece, piece, ag_s.at[owner], ag_r.at[owner], owner, rep).wait_recv()
            copy(piece, piece, fwd_s.at[owner], fwd_r.at[owner], me, 1 - rep).start()

        return carry

    lax.fori_loop(1, parts, pass_on, 0)

    def land(k, carry):
        piece = full.at[1 - rep, k]
        copy(piece, piece, fwd_s.at[k], fwd_r.at[k], me, 1 - rep).wait_recv()
        return carry

    lax.fori_loop(0, owners, land, 0)
    for k in range(owners):
        height = min(chunk, width - k * chunk)
        gs_out[k * chunk : k * chunk + height, :] = full[0, k, :height, :].astype(F32)
        gn_out[k * chunk : k * chunk + height, :] = full[1, k, :height, :].astype(F32)

    all_done(lambda k: bnd_out.at[k], bnd_in, bnd_s, bnd_r)
    all_done(lambda k: ret_out.at[k], ret_in, ret_s, ret_r)
    all_done(lambda k: rs_out.at[k], rs_in, rs_s, rs_r, owners)
    all_done(lambda k: loss_buf.at[me], loss_buf, los_s, los_r)
    mirror.wait_send()
    for c in idx_copies:
        c.wait_send()
    for c in hid_copies.values():
        c.wait_send()

    @pl.when(me < owners)
    def _():
        def sent(k, carry):
            peer = at(k)
            piece = full.at[rep, me]
            copy(piece, piece, ag_s.at[peer], ag_r.at[me], peer, rep).wait_send()
            return carry

        lax.fori_loop(1, parts, sent, 0)

    def forwarded(k, carry):
        piece = full.at[rep, k]
        copy(piece, piece, fwd_s.at[k], fwd_r.at[k], me, 1 - rep).wait_send()
        return carry

    lax.fori_loop(0, owners, forwarded, 0)


def on_device(
    node_feats,
    w_self,
    w_neigh,
    neighbour_index,
    neighbour_count,
    send_index,
    send_count,
    edge_src,
    edge_dst,
    tile_count,
    neg_rows,
):
    partitions = lax.axis_size("dom")
    replicas = lax.axis_size("rep")
    node_rows, width = node_feats.shape
    fan_out = neighbour_index.shape[1]
    slot_cap = send_index.shape[2]
    window = edge_src.shape[1]
    edge_here = edge_src.shape[2]
    neg_parts = neg_rows.shape[2] // edge_here
    remote = partitions * slot_cap
    table = node_rows + remote
    position = jnp.arange(edge_here, dtype=jnp.int32)
    filled = jnp.repeat(tile_count[0], 128, axis=1, total_repeat_length=edge_here)
    live_src = jnp.where(position % 128 < filled, edge_src[0], -1)
    packed = jnp.concatenate(
        [
            live_src[:, None],
            edge_dst[0][:, None],
            neg_rows[0].reshape(window, neg_parts, edge_here),
        ],
        axis=1,
    )
    packed = jnp.pad(packed, ((0, 0), (0, -packed.shape[1] % 8), (0, 0)))
    fan = jnp.arange(fan_out, dtype=jnp.int32)[None, :]
    nidx = jnp.where(fan < neighbour_count[:, None], neighbour_index, -1)
    slot_live = jnp.arange(slot_cap, dtype=jnp.int32)[None, :] < send_count[0][:, None]
    picks = jnp.where(slot_live, send_index[0], -1).reshape(-1)
    chunk = -(-width // partitions)
    chunk = -(-chunk // 16) * 16
    owners = -(-width // chunk)
    vmem = pl.BlockSpec(memory_space=pltpu.VMEM)
    dma = pltpu.SemaphoreType.DMA
    outs = pl.pallas_call(
        functools.partial(step_kernel, partitions, neg_parts),
        out_shape=(
            jax.ShapeDtypeStruct((8, 128), F32),
            jax.ShapeDtypeStruct((node_rows, width), F32),
            jax.ShapeDtypeStruct((width, width), F32),
            jax.ShapeDtypeStruct((width, width), F32),
        ),
        in_specs=[vmem] * 9,
        out_specs=(vmem,) * 4,
        scratch_shapes=[
            pltpu.VMEM((partitions, slot_cap, width), BF16),
            pltpu.VMEM((partitions, slot_cap, width), BF16),
            pltpu.VMEM((partitions, slot_cap, width), BF16),
            pltpu.VMEM((partitions, slot_cap, width), BF16),
            pltpu.VMEM(packed.shape, jnp.int32),
            pltpu.VMEM((window, 2) + packed.shape[1:], jnp.int32),
            pltpu.VMEM((node_rows, width), BF16),
            pltpu.VMEM((window, node_rows, width), BF16),
            pltpu.VMEM((window, node_rows, node_rows), F32),
            pltpu.VMEM((window, node_rows, node_rows), F32),
            pltpu.VMEM((window, node_rows, node_rows), F32),
            pltpu.VMEM((window, node_rows, node_rows), F32),
            pltpu.VMEM((node_rows, table), BF16),
            pltpu.VMEM((table, node_rows), BF16),
            pltpu.VMEM((node_rows, width), BF16),
            pltpu.VMEM((node_rows, width), BF16),
            pltpu.VMEM((owners, chunk, width), BF16),
            pltpu.VMEM((partitions, chunk, width), BF16),
            pltpu.VMEM((2, owners, chunk, width), BF16),
            pltpu.VMEM((partitions, 8, 128), F32),
            pltpu.VMEM((node_rows, width), F32),
            dma((partitions,)),
            dma((partitions,)),
            dma((partitions,)),
            dma((partitions,)),
            dma,
            dma,
            dma((window - 1, 2)),
            dma((window - 1, 2)),
            dma((window,)),
            dma((window,)),
            dma((partitions,)),
            dma((partitions,)),
            dma((partitions,)),
            dma((partitions,)),
            dma((owners,)),
            dma((owners,)),
            dma((partitions,)),
            dma((partitions,)),
        ],
        compiler_params=pltpu.CompilerParams(
            collective_id=0, has_side_effects=True, vmem_limit_bytes=48 * 1024 * 1024
        ),
    )(
        node_feats,
        w_self,
        w_neigh,
        nidx,
        nidx.T,
        neighbour_count.astype(F32)[:, None],
        picks[None, :],
        picks[:, None],
        packed,
    )
    loss_tile, grad_x, grad_self, grad_neigh = outs
    loss = loss_tile[0, 0] / float(partitions * window * edge_here * replicas)
    return (loss, grad_x, grad_self, grad_neigh)


def solution(mesh):
    in_specs = (
        P("dom", None),
        P(),
        P(),
        P("dom", None),
        P("dom"),
        P("dom", None, None),
        P("dom", None),
        P("dom", None, "rep"),
        P("dom", None, "rep"),
        P("dom", None, "rep"),
        P("dom", None, None),
    )
    out_specs = (P(), P("dom", None), P(), P())
    return jax.shard_map(
        on_device, mesh=mesh, in_specs=in_specs, out_specs=out_specs, check_vma=False
    )
```
